32 devices in a mesh: grp: 4 (over z), mem: 8 (over y, x, core).
Axes of the slice: x: 2, y: 2, z: 4, core: 2. Of those that a mesh axis runs over, the one named last changes fastest.
Arguments:
- volume: float32 [4, 8, 8, 512, 1024], P('grp', 'mem'), may hold values from -1 to 1
- transfer_coef: float32 [4, 4], replicated, may hold values from -3 to 3
- group_order: int32 [4], replicated, may hold values from 0 to 3, each once
- member_order: int32 [4, 8], replicated, may hold values from 0 to 7, each once within a row
- active_mask: int32 [4, 8], P('grp', 'mem'), may hold values 0 or 1
Outputs:
- picture: float32 [4, 512, 1024], P(None, 'mem', 'grp')
The draws below stay inside these ranges and needn't reach their ends.
All inputs are finite; a program needn't handle non-finite values. No bound on the sum of `active_mask` on one device may be relied on, other than what follows from the above.
Results may differ from the reference program's by a relative error of at most 0.0003.
Values sent between devices are 32-bit elements; how exact they have to be, the bound alone decides.
A program may use at most 192 MiB of HBM per device.

```python
import jax
import jax.numpy as jnp
from jax import lax

SAMPLES = 8
ROWS = 512
COLS = 1024
N_GRP = 4
N_MEM = 8


def touch_ends(result, own_key, smallest, top_value):
    longest = result.shape.index(max(result.shape))
    spots = []
    for shift in (0, 1):
        where = [jax.random.randint(jax.random.fold_in(own_key, axis), (), 0, length) for axis, length in enumerate(result.shape)]
        where[longest] = (where[longest] + shift) % result.shape[longest]
        spots.append(tuple(where))
    return result.at[spots[0]].set(smallest).at[spots[1]].set(top_value)


def steps_of(stream_key, dims, shards, low, top_value):
    loudness, own = 1.0, jax.random.fold_in(stream_key, 6)
    for axis_at, shards_of in shards:
        steps = jnp.exp(jax.random.uniform(jax.random.fold_in(own, axis_at), (shards_of,), jnp.float32, low / len(shards), top_value / len(shards)))
        loudness = loudness * jnp.repeat(steps, dims[axis_at] // shards_of).reshape([-1 if axis == axis_at else 1 for axis in range(len(dims))])
    return loudness


def gaussian(stream_key, extent, width, reach, kind=jnp.bfloat16):
    values = jax.random.normal(stream_key, extent, jnp.float32) * width
    return jnp.minimum(jnp.maximum(values, -reach), reach).astype(kind)


def setup_inputs(seed: int = 0) -> dict:
    key_of = jax.random.split(jax.random.key(seed), 6)
    return {
        "volume": jnp.clip(jax.random.uniform(key_of[0], (N_GRP, N_MEM, SAMPLES, ROWS, COLS), jnp.float32, -1.0, 1.0) * steps_of(key_of[0], (N_GRP, N_MEM, SAMPLES, ROWS, COLS), ((0, 4), (1, 8)), -0.4, 0.0), -1.0, 1.0),
        "transfer_coef": gaussian(key_of[1], (4, 4), 0.6, 3.0, jnp.float32),
        "group_order": jax.random.permutation(key_of[2], N_GRP).astype(jnp.int32),
        "member_order": jax.vmap(lambda own: jax.random.permutation(own, N_MEM))(jax.random.split(key_of[3], N_GRP)).reshape((N_GRP, N_MEM)).astype(jnp.int32),
        "active_mask": touch_ends((jax.random.randint(key_of[4], (N_GRP, N_MEM), 0, 4) < 3).astype(jnp.int32), jax.random.fold_in(key_of[4], 1), 0, 1),
    }


def polynomial(coef_row, values):
    return coef_row[0] + values * (coef_row[1] + values * (coef_row[2] + values * coef_row[3]))


def march_brick(samples, transfer_coef, active_flag):
    density_scale = 3.0 / (SAMPLES * N_GRP * N_MEM)

    def march_step(state_pair, values):
        optical_depth, colour = state_pair
        extinction = polynomial(transfer_coef[3], values) ** 2 * density_scale
        opacity = 1.0 - jnp.exp(-extinction)
        tinted = jax.nn.sigmoid(jnp.stack([polynomial(transfer_coef[channel], values) for channel in range(3)]))
        colour = colour + (jnp.exp(-optical_depth) * opacity)[None] * tinted
        return (optical_depth + extinction, colour), None

    start = (jnp.zeros(samples.shape[1:], jnp.float32), jnp.zeros((3,) + samples.shape[1:], jnp.float32))
    (optical_depth, colour), unused = lax.scan(march_step, start, samples)
    coverage = 1.0 - jnp.exp(-optical_depth)
    return jnp.concatenate([colour, coverage[None]], 0) * active_flag


def reference(volume, transfer_coef, group_order, member_order, active_mask):
    global_rank = (group_order[:, None] * N_MEM + member_order).reshape(-1).astype(jnp.int32)
    total = N_GRP * N_MEM
    positions = jnp.arange(total, dtype=jnp.int32)
    inverse = jnp.sum(positions[:, None] * (global_rank[:, None] == positions[None, :]).astype(jnp.int32), axis=0).astype(jnp.int32)

    def composite_step(picture, brick_index):
        group_index = brick_index // N_MEM
        member_index = brick_index % N_MEM
        samples = volume[group_index, member_index]
        active_flag = active_mask[group_index, member_index].astype(jnp.float32)
        layer = march_brick(samples, transfer_coef, active_flag)
        return picture + (1.0 - picture[3:4]) * layer, None

    picture, unused = lax.scan(composite_step, jnp.zeros((4, ROWS, COLS), jnp.float32), inverse)
    return picture
```

```python
import functools
import math

import jax
import jax.numpy as jnp
from jax import lax
from jax.experimental import pallas as pl
from jax.experimental.pallas import tpu as pltpu
from jax.sharding import PartitionSpec as P

MESH = pl.DeviceIdType.MESH
CHUNKS = 8
EARLY = 6
TILE_ROWS = 8


def kernel(groups, members, coef_ref, group_ref, member_ref, active_ref, volume_ref, out_ref,
           vol, tloc, tin, col, pcol, mout, min_, tnear, tslab, sout, sin, zout, zin,
           vol_sem, t_send, t_recv, c_send, c_recv, m_send, m_recv, s_send, s_recv, z_send, z_recv):
    chunks, _, samples, rows, cols = vol.shape
    block_rows = chunks * rows
    chips = members // 2
    group_cols = cols // groups
    g = lax.axis_index("grp")
    me = lax.axis_index("mem")
    chip = me // 2
    core = me % 2
    partner = me + 1 - 2 * core
    row_tiles = rows // TILE_ROWS

    def fetch(j, d):
        start = pl.multiple_of(d * block_rows + j * rows, TILE_ROWS)
        return pltpu.make_async_copy(
            volume_ref.at[0, 0, :, pl.ds(start, rows), :], vol.at[j, d], vol_sem.at[j])

    def send_t(j, d, src):
        return pltpu.make_async_remote_copy(
            tloc.at[j, d], tin.at[j, src], t_send, t_recv.at[j],
            device_id={"mem": d}, device_id_type=MESH)

    def send_col(j, k):
        return pltpu.make_async_remote_copy(
            col.at[j, 2 * k + 1 - core], pcol.at[j, k], c_send, c_recv.at[j],
            device_id={"mem": partner}, device_id_type=MESH)

    def send_m(j, k, src):
        return pltpu.make_async_remote_copy(
            mout.at[j, k], min_.at[j, src], m_send, m_recv.at[j],
            device_id={"mem": 2 * k + core}, device_id_type=MESH)

    def send_s(j, k, src):
        return pltpu.make_async_remote_copy(
            sout.at[j, k], sin.at[j, src], s_send, s_recv.at[j],
            device_id={"mem": 2 * k + core}, device_id_type=MESH)

    def send_z(j, k, src):
        return pltpu.make_async_remote_copy(
            zout.at[j, k], zin.at[j, src], z_send, z_recv.at[j],
            device_id={"grp": k}, device_id_type=MESH)

    def landed(ref, sem):
        pltpu.make_async_copy(ref, ref, sem).wait()

    def each(count, fn):
        def step(i, carry):
            fn(i)
            return carry
        lax.fori_loop(0, count, step, 0)

    each(chunks, lambda j: each(members, lambda off: fetch(j, (me + 1 + off) % members).start()))

    barrier = pltpu.get_barrier_semaphore()
    each(members - 1, lambda off: pl.semaphore_signal(
        barrier, inc=1, device_id={"mem": (me + 1 + off) % members}, device_id_type=MESH))
    each(groups - 1, lambda off: pl.semaphore_signal(
        barrier, inc=1, device_id={"grp": (g + 1 + off) % groups}, device_id_type=MESH))

    density_factor = math.sqrt(3.0 / (samples * groups * members) * math.log2(math.e))
    coef = [[coef_ref[c, p] * (0.5 if c < 3 else density_factor) for p in range(4)] for c in range(4)]
    active = active_ref[0, 0].astype(jnp.float32)
    half_active = active * 0.5
    width = min(512, cols)
    col_tiles = cols // width
    ranks = [member_ref[g, i] for i in range(members)]
    near = [jnp.minimum(ranks[2 * q], ranks[2 * q + 1]) for q in range(chips)]
    far = [jnp.maximum(ranks[2 * q], ranks[2 * q + 1]) for q in range(chips)]
    own_first = member_ref[g, me] < member_ref[g, partner]
    orders = [group_ref[i] for i in range(groups)]

    def tiles(fn, count=None):
        def step(i, carry):
            row = pl.ds(pl.multiple_of((i // col_tiles) * TILE_ROWS, TILE_ROWS), TILE_ROWS)
            column = pl.ds(pl.multiple_of((i % col_tiles) * width, width), width)
            fn(row, column)
            return carry
        lax.fori_loop(0, row_tiles * col_tiles, step, 0)

    def march(j, d):
        def tile(row, column):
            depth = jnp.zeros((TILE_ROWS, width), jnp.float32)
            light = jnp.ones((TILE_ROWS, width), jnp.float32)
            colour = [jnp.zeros((TILE_ROWS, width), jnp.float32) for _ in range(3)]
            for k in range(samples):
                v = vol[j, d, k, row, column]
                poly = [q[0] + v * (q[1] + v * (q[2] + v * q[3])) for q in coef]
                depth = depth - poly[3] * poly[3]
                after = jnp.exp2(depth)
                weight = light - after
                light = after
                colour = [colour[c] + weight * jnp.tanh(poly[c]) for c in range(3)]
            coverage = 1.0 - light
            tloc[j, d, row, column] = 1.0 - active * coverage
            for c in range(3):
                col[j, d, c, row, column] = half_active * (coverage + colour[c])
        tiles(tile)

    early = min(EARLY, members - 1)

    def produce(j):
        @pl.when(j > 0)
        def _():
            landed(vol.at[j], vol_sem.at[j])

        def unit(off):
            d = (me + 1 + off) % members

            @pl.when(jnp.logical_or(j > 0, off >= early))
            def _():
                march(j, d)

            @pl.when(off < members - 1)
            def _():
                send_t(j, d, me).start()

            @pl.when(d % 2 != core)
            def _():
                send_col(j, d // 2).start()
        each(members, unit)

        def keep(row, column):
            tin[j, me, row, column] = tloc[j, me, row, column]
        tiles(keep)

    def ratios(j):
        landed(tin.at[j, pl.ds(0, members - 1)], t_recv.at[j])

        def tile(row, column):
            t = [tin[j, i, row, column] for i in range(members)]
            total = t[0]
            for i in range(1, members):
                total = total * t[i]
            tslab[j, row, column] = total
            for q in range(chips):
                before = jnp.ones((TILE_ROWS, width), jnp.float32)
                between = jnp.ones((TILE_ROWS, width), jnp.float32)
                for i in range(members):
                    nearer = ranks[i] < near[q]
                    inside = jnp.logical_and(ranks[i] >= near[q], ranks[i] < far[q])
                    before = before * jnp.where(nearer, t[i], 1.0)
                    between = between * jnp.where(inside, t[i], 1.0)
                tnear[j, q, row, column] = before
                mout[j, q, row, column] = between
        tiles(tile)
        each(chips - 1, lambda off: send_m(j, (chip + 1 + off) % chips, chip).start())

        def keep(row, column):
            min_[j, chip, row, column] = mout[j, chip, row, column]
        tiles(keep)

    def pair_sums(j):
        landed(min_.at[j, pl.ds(0, chips - 1)], m_recv.at[j])
        landed(pcol.at[j], c_recv.at[j])

        def unit(off):
            k = (chip + 1 + off) % chips

            def tile(row, column):
                ratio = min_[j, k, row, column]
                own_factor = jnp.where(own_first, 1.0, ratio)
                other_factor = jnp.where(own_first, ratio, 1.0)
                for c in range(3):
                    sout[j, k, c, row, column] = (
                        col[j, 2 * k + core, c, row, column] * own_factor
                        + pcol[j, k, c, row, column] * other_factor)
            tiles(tile)

            @pl.when(off < chips - 1)
            def _():
                send_s(j, k, chip).start()
        each(chips, unit)

        def keep(row, column):
            for c in range(3):
                sin[j, chip, c, row, column] = sout[j, chip, c, row, column]
        tiles(keep)

    def slab(j):
        landed(sin.at[j, pl.ds(0, chips - 1)], s_recv.at[j])

        def part(k):
            def tile(i):
                row = pl.ds(pl.multiple_of(i * TILE_ROWS, TILE_ROWS), TILE_ROWS)
                column = pl.ds(pl.multiple_of(k * group_cols, group_cols), group_cols)
                factor = [tnear[j, q, row, column] for q in range(chips)]
                for c in range(3):
                    total = factor[0] * sin[j, 0, c, row, column]
                    for q in range(1, chips):
                        total = total + factor[q] * sin[j, q, c, row, column]
                    zout[j, k, c, row, :] = total
                zout[j, k, 3, row, :] = tslab[j, row, column]
            each(row_tiles, tile)

        def unit(off):
            k = (g + 1 + off) % groups
            part(k)

            @pl.when(off < groups - 1)
            def _():
                send_z(j, k, g).start()
        each(groups, unit)
        zin[j, g] = zout[j, g]

    def finish(j):
        landed(zin.at[j, pl.ds(0, groups - 1)], z_recv.at[j])
        for r in range(row_tiles):
            row = pl.ds(r * TILE_ROWS, TILE_ROWS)
            out_row = pl.ds(pl.multiple_of(j * rows + r * TILE_ROWS, TILE_ROWS), TILE_ROWS)
            t = [zin[j, i, 3, row, :] for i in range(groups)]
            total = t[0]
            for i in range(1, groups):
                total = total * t[i]
            out_ref[3, out_row, :] = 1.0 - total
            factor = []
            for i in range(groups):
                before = jnp.ones_like(total)
                for o in range(groups):
                    if o != i:
                        before = before * jnp.where(orders[o] < orders[i], t[o], 1.0)
                factor.append(before)
            for c in range(3):
                colour = factor[0] * zin[j, 0, c, row, :]
                for i in range(1, groups):
                    colour = colour + factor[i] * zin[j, i, c, row, :]
                out_ref[c, out_row, :] = colour

    def step(s):
        for lag, stage in enumerate((produce, ratios, pair_sums, slab, finish)):
            @pl.when(jnp.logical_and(s >= lag, s < chunks + lag))
            def _():
                stage(s - lag)
    landed(vol.at[0], vol_sem.at[0])
    each(early, lambda off: march(0, (me + 1 + off) % members))
    pl.semaphore_wait(barrier, members + groups - 2)
    each(chunks + 4, step)

    landed(tloc.at[:, pl.ds(0, members - 1)], t_send)
    landed(pcol, c_send)
    landed(mout.at[:, pl.ds(0, chips - 1)], m_send)
    landed(sout.at[:, pl.ds(0, chips - 1)], s_send)
    landed(zout.at[:, pl.ds(0, groups - 1)], z_send)


def solution(mesh):
    groups, members = mesh.shape["grp"], mesh.shape["mem"]
    chips = members // 2

    def body(volume, transfer_coef, group_order, member_order, active_mask):
        samples, image_rows, cols = volume.shape[2:]
        block_rows = image_rows // members
        chunks = min(CHUNKS, block_rows // TILE_ROWS)
        rows = block_rows // chunks
        group_cols = cols // groups
        smem = pl.BlockSpec(memory_space=pltpu.SMEM)
        f32 = jnp.float32
        dma = pltpu.SemaphoreType.DMA
        scratch = [
            pltpu.VMEM((chunks, members, samples, rows, cols), f32),
            pltpu.VMEM((chunks, members, rows, cols), f32),
            pltpu.VMEM((chunks, members, rows, cols), f32),
            pltpu.VMEM((chunks, members, 3, rows, cols), f32),
            pltpu.VMEM((chunks, chips, 3, rows, cols), f32),
            pltpu.VMEM((chunks, chips, rows, cols), f32),
            pltpu.VMEM((chunks, chips, rows, cols), f32),
            pltpu.VMEM((chunks, chips, rows, cols), f32),
            pltpu.VMEM((chunks, rows, cols), f32),
            pltpu.VMEM((chunks, chips, 3, rows, cols), f32),
            pltpu.VMEM((chunks, chips, 3, rows, cols), f32),
            pltpu.VMEM((chunks, groups, 4, rows, group_cols), f32),
            pltpu.VMEM((chunks, groups, 4, rows, group_cols), f32),
            dma((chunks,)),
            dma, dma((chunks,)),
            dma, dma((chunks,)),
            dma, dma((chunks,)),
            dma, dma((chunks,)),
            dma, dma((chunks,)),
        ]
        return pl.pallas_call(
            functools.partial(kernel, groups, members),
            out_shape=pltpu.VMEM((4, block_rows, group_cols), f32),
            in_specs=[smem, smem, smem, smem, pl.BlockSpec(memory_space=pl.ANY)],
            out_specs=pl.BlockSpec(memory_space=pltpu.VMEM),
            scratch_shapes=scratch,
            compiler_params=pltpu.CompilerParams(
                collective_id=0, has_side_effects=True, vmem_limit_bytes=60 * 1024 * 1024),
        )(transfer_coef, group_order, member_order, active_mask, volume)

    in_specs = (P("grp", "mem", None, None, None), P(), P(), P(), P("grp", "mem"))
    out_specs = P(None, "mem", "grp")
    return jax.shard_map(body, mesh=mesh, in_specs=in_specs, out_specs=out_specs, check_vma=False)
```

```python
import functools
import math

import jax
import jax.numpy as jnp
from jax import lax
from jax.experimental import pallas as pl
from jax.experimental.pallas import tpu as pltpu
from jax.sharding import PartitionSpec as P

MESH = pl.DeviceIdType.MESH
TILE_ROWS = 8
LANES = 128
HALVES = 2
EARLY = 2
LAGS = (0, 6, 7, 8, 9, 10)


def kernel(groups, members, coef_ref, group_ref, member_ref, active_ref, volume_ref, out_ref,
           vol, tloc, tin, col, pcol, rout, rin, qout, qin, tfirst, tslab, aout, ain, own, bout, bin_,
           zout, zin, vol_sem, t_send, t_recv, c_send, c_recv, r_send, r_recv, q_send, q_recv,
           a_send, a_recv, b_send, b_recv, z_send, z_recv):
    chunks, _, rows, cols = tloc.shape
    stripes, _, samples, _, _ = vol.shape
    block_rows = stripes * rows
    halves = chunks // stripes
    part = cols // groups
    group_cols = part * halves
    chips = members // 2
    pairs = chips // 2
    g = lax.axis_index("grp")
    me = lax.axis_index("mem")
    chip = me // 2
    core = me % 2
    partner = me + 1 - 2 * core

    side = (1 - core) * ((chip // 2) % 2) + core * (chip % 2)
    mate = chip + (1 - core) * (2 - 4 * ((chip // 2) % 2)) + core * (1 - 2 * (chip % 2))
    my_pair = (1 - core) * ((chip // 4) * 2 + chip % 2) + core * (chip // 2)

    def member_of_pair(p, which):
        return (1 - core) * ((p // 2) * 4 + 2 * which + p % 2) + core * (2 * p + which)

    def fetch(j, d):
        start = pl.multiple_of(d * block_rows + j * rows, TILE_ROWS)
        return pltpu.make_async_copy(
            volume_ref.at[0, 0, :, pl.ds(start, rows), :], vol.at[j, d], vol_sem.at[j])

    def send(src, dst, send_sem, recv_sem, device):
        pltpu.make_async_remote_copy(
            src, dst, send_sem, recv_sem, device_id=device, device_id_type=MESH).start()

    def landed(ref, sem):
        pltpu.make_async_copy(ref, ref, sem).wait()

    def each(count, fn):
        def step(i, carry):
            fn(i)
            return carry
        lax.fori_loop(0, count, step, 0)

    each(stripes, lambda j: each(members, lambda off: fetch(j, (me + 1 + off) % members).start()))

    barrier = pltpu.get_barrier_semaphore()
    each(members - 1, lambda off: pl.semaphore_signal(
        barrier, inc=1, device_id={"mem": (me + 1 + off) % members}, device_id_type=MESH))
    each(groups - 1, lambda off: pl.semaphore_signal(
        barrier, inc=1, device_id={"grp": (g + 1 + off) % groups}, device_id_type=MESH))

    density_factor = math.sqrt(3.0 / (samples * groups * members) * math.log2(math.e))
    coef = [[coef_ref[c, p] * (0.5 if c < 3 else density_factor) for p in range(4)] for c in range(4)]
    active = active_ref[0, 0].astype(jnp.float32)
    half_active = active * 0.5
    width = min(512, cols)
    piece = min(part, width)
    ranks = [member_ref[g, i] for i in range(members)]
    near = [jnp.minimum(ranks[2 * q], ranks[2 * q + 1]) for q in range(chips)]
    far = [jnp.maximum(ranks[2 * q], ranks[2 * q + 1]) for q in range(chips)]
    orders = [group_ref[i] for i in range(groups)]

    def rank_of(member):
        return member_ref[g, member]

    def chip_rank(q):
        return jnp.minimum(rank_of(2 * q), rank_of(2 * q + 1))

    own_first = rank_of(me) < rank_of(partner)
    chip_first = chip_rank(chip) < chip_rank(mate)

    def tiles(fn):
        def step(i):
            fn(pl.ds(pl.multiple_of(i * width, width), width))
        if cols == width:
            fn(slice(None))
        else:
            each(cols // width, step)

    def march(i, d):
        j, h = i // halves, i % halves

        def tile(t):
            depth = jnp.zeros((TILE_ROWS, width), jnp.float32)
            light = jnp.ones((TILE_ROWS, width), jnp.float32)
            colour = [jnp.zeros((TILE_ROWS, width), jnp.float32) for _ in range(3)]
            starts = []
            for u in range(width // piece):
                at = t * width + u * piece
                starts.append(pl.multiple_of((at // part) * group_cols + h * part + at % part, LANES))
            column = pl.ds(pl.multiple_of(t * width, LANES), width)
            for k in range(samples):
                v = jnp.concatenate([vol[j, d, k, :, pl.ds(s, piece)] for s in starts], axis=1)
                poly = [q[0] + v * (q[1] + v * (q[2] + v * q[3])) for q in coef]
                depth = depth - poly[3] * poly[3]
                after = jnp.exp2(depth)
                weight = light - after
                light = after
                colour = [colour[c] + weight * jnp.tanh(poly[c]) for c in range(3)]
            coverage = 1.0 - light
            tloc[i, d, :, column] = 1.0 - active * coverage
            for c in range(3):
                col[i, d, c, :, column] = half_active * (coverage + colour[c])
        if cols == width:
            tile(0)
        else:
            each(cols // width, tile)

    early = min(EARLY, chunks)

    def wait_volume(i):
        @pl.when(i % halves == 0)
        def _():
            landed(vol.at[i // halves], vol_sem.at[i // halves])

    def produce(i):
        @pl.when(i >= early)
        def _():
            wait_volume(i)

        def unit(off):
            d = (me + 1 + off) % members

            @pl.when(i >= early)
            def _():
                march(i, d)

            @pl.when(off < members - 1)
            def _():
                send(tloc.at[i, d], tin.at[i, me], t_send, t_recv.at[i], {"mem": d})

            @pl.when(d % 2 != core)
            def _():
                send(col.at[i, d], pcol.at[i, d // 2], c_send, c_recv.at[i], {"mem": partner})
        each(members, unit)
        tin[i, me] = tloc[i, me]

    def ratios(i):
        landed(tin.at[i, pl.ds(0, members - 1)], t_recv.at[i])

        def tile(column):
            t = [tin[i, m, :, column] for m in range(members)]
            one = jnp.ones((TILE_ROWS, width), jnp.float32)
            total = t[0]
            for m in range(1, members):
                total = total * t[m]
            tslab[i, :, column] = total

            def between(low, high):
                product = one
                for m in range(members):
                    inside = ranks[m] < high
                    if low is not None:
                        inside = jnp.logical_and(ranks[m] >= low, inside)
                    product = product * jnp.where(inside, t[m], 1.0)
                return product

            for q in range(chips):
                rout[i, q, :, column] = between(near[q], far[q])
            for p in range(pairs):
                a, b = chip_rank(member_of_pair(p, 0)), chip_rank(member_of_pair(p, 1))
                first, second = jnp.minimum(a, b), jnp.maximum(a, b)
                tfirst[i, p, :, column] = between(None, first)
                qout[i, p, :, column] = between(first, second)
        tiles(tile)

        def to_chip(off):
            k = (chip + 1 + off) % chips
            send(rout.at[i, k], rin.at[i, chip], r_send, r_recv.at[i], {"mem": 2 * k + core})
        each(chips - 1, to_chip)

        def to_pair(off):
            p = (my_pair + 1 + off) % pairs
            send(qout.at[i, p], qin.at[i, my_pair], q_send, q_recv.at[i],
                 {"mem": 2 * member_of_pair(p, side) + core})
        each(pairs - 1, to_pair)
        rin[i, chip] = rout[i, chip]
        qin[i, my_pair] = qout[i, my_pair]

    def chip_sums(i):
        landed(rin.at[i, pl.ds(0, chips - 1)], r_recv.at[i])
        landed(pcol.at[i], c_recv.at[i])

        def sums(k, ref, p):
            def tile(column):
                ratio = rin[i, k, :, column]
                own_factor = jnp.where(own_first, 1.0, ratio)
                other_factor = jnp.where(own_first, ratio, 1.0)
                for c in range(3):
                    ref[i, p, c, :, column] = (
                        col[i, 2 * k + core, c, :, column] * own_factor
                        + pcol[i, k, c, :, column] * other_factor)
            tiles(tile)
        each(pairs, lambda p: sums(member_of_pair(p, 1 - side), aout, p))
        send(aout.at[i], ain.at[i], a_send, a_recv.at[i], {"mem": 2 * mate + core})
        each(pairs, lambda p: sums(member_of_pair(p, side), own, p))

    def pair_sums(i):
        landed(ain.at[i], a_recv.at[i])
        if pairs > 1:
            landed(qin.at[i, pl.ds(0, pairs - 1)], q_recv.at[i])

        def unit(off):
            p = (my_pair + 1 + off) % pairs

            def tile(column):
                ratio = qin[i, p, :, column]
                own_factor = jnp.where(chip_first, 1.0, ratio)
                other_factor = jnp.where(chip_first, ratio, 1.0)
                for c in range(3):
                    bout[i, p, c, :, column] = (
                        own[i, p, c, :, column] * own_factor + ain[i, p, c, :, column] * other_factor)
            tiles(tile)

            @pl.when(off < pairs - 1)
            def _():
                send(bout.at[i, p], bin_.at[i, my_pair], b_send, b_recv.at[i],
                     {"mem": 2 * member_of_pair(p, side) + core})
        each(pairs, unit)
        bin_[i, my_pair] = bout[i, my_pair]

    def slab(i):
        if pairs > 1:
            landed(bin_.at[i, pl.ds(0, pairs - 1)], b_recv.at[i])
        for k in range(groups):
            column = pl.ds(k * part, part)
            factor = [tfirst[i, p, :, column] for p in range(pairs)]
            for c in range(3):
                total = factor[0] * bin_[i, 0, c, :, column]
                for p in range(1, pairs):
                    total = total + factor[p] * bin_[i, p, c, :, column]
                zout[i, k, c] = total
            zout[i, k, 3] = tslab[i, :, column]

        def unit(off):
            k = (g + 1 + off) % groups
            send(zout.at[i, k], zin.at[i, g], z_send, z_recv.at[i], {"grp": k})
        each(groups - 1, unit)
        zin[i, g] = zout[i, g]

    def finish(i):
        landed(zin.at[i, pl.ds(0, groups - 1)], z_recv.at[i])
        row = pl.ds(pl.multiple_of((i // halves) * TILE_ROWS, TILE_ROWS), TILE_ROWS)
        column = pl.ds(pl.multiple_of((i % halves) * part, LANES), part)
        t = [zin[i, k, 3] for k in range(groups)]
        total = t[0]
        for k in range(1, groups):
            total = total * t[k]
        out_ref[3, row, column] = 1.0 - total
        factor = []
        for k in range(groups):
            before = jnp.ones_like(total)
            for o in range(groups):
                if o != k:
                    before = before * jnp.where(orders[o] < orders[k], t[o], 1.0)
            factor.append(before)
        for c in range(3):
            colour = factor[0] * zin[i, 0, c]
            for k in range(1, groups):
                colour = colour + factor[k] * zin[i, k, c]
            out_ref[c, row, column] = colour

    stages = (produce, ratios, chip_sums, pair_sums, slab, finish)

    def step(s):
        for lag, stage in zip(LAGS, stages):
            @pl.when(jnp.logical_and(s >= lag, s < chunks + lag))
            def _():
                stage(s - lag)

    def first(i):
        wait_volume(i)
        each(members, lambda off: march(i, (me + 1 + off) % members))
    each(early, first)
    pl.semaphore_wait(barrier, members + groups - 2)
    each(chunks + LAGS[-1], step)

    landed(tloc.at[:, pl.ds(0, members - 1)], t_send)
    landed(pcol, c_send)
    landed(rout.at[:, pl.ds(0, chips - 1)], r_send)
    if pairs > 1:
        landed(qout.at[:, pl.ds(0, pairs - 1)], q_send)
        landed(bout.at[:, pl.ds(0, pairs - 1)], b_send)
    landed(aout, a_send)
    landed(zout.at[:, pl.ds(0, groups - 1)], z_send)


def solution(mesh):
    groups, members = mesh.shape["grp"], mesh.shape["mem"]
    chips = members // 2
    pairs = chips // 2

    def body(volume, transfer_coef, group_order, member_order, active_mask):
        samples, image_rows, cols = volume.shape[2:]
        block_rows = image_rows // members
        stripes = block_rows // TILE_ROWS
        group_cols = cols // groups
        halves = min(HALVES, group_cols // LANES)
        part = group_cols // halves
        wide = part * groups
        chunks = stripes * halves
        smem = pl.BlockSpec(memory_space=pltpu.SMEM)
        dma = pltpu.SemaphoreType.DMA

        def vmem(*shape):
            return pltpu.VMEM(shape, jnp.float32)

        tile = (TILE_ROWS, wide)
        scratch = [
            vmem(stripes, members, samples, TILE_ROWS, cols),
            vmem(chunks, members, *tile),
            vmem(chunks, members, *tile),
            vmem(chunks, members, 3, *tile),
            vmem(chunks, chips, 3, *tile),
            vmem(chunks, chips, *tile),
            vmem(chunks, chips, *tile),
            vmem(chunks, pairs, *tile),
            vmem(chunks, pairs, *tile),
            vmem(chunks, pairs, *tile),
            vmem(chunks, *tile),
            vmem(chunks, pairs, 3, *tile),
            vmem(chunks, pairs, 3, *tile),
            vmem(chunks, pairs, 3, *tile),
            vmem(chunks, pairs, 3, *tile),
            vmem(chunks, pairs, 3, *tile),
            vmem(chunks, groups, 4, TILE_ROWS, part),
            vmem(chunks, groups, 4, TILE_ROWS, part),
            dma((stripes,)),
        ]
        for _ in range(7):
            scratch += [dma, dma((chunks,))]
        return pl.pallas_call(
            functools.partial(kernel, groups, members),
            out_shape=pltpu.VMEM((4, block_rows, group_cols), jnp.float32),
            in_specs=[smem, smem, smem, smem, pl.BlockSpec(memory_space=pl.ANY)],
            out_specs=pl.BlockSpec(memory_space=pltpu.VMEM),
            scratch_shapes=scratch,
            compiler_params=pltpu.CompilerParams(
                collective_id=0, has_side_effects=True, vmem_limit_bytes=60 * 1024 * 1024),
        )(transfer_coef, group_order, member_order, active_mask, volume)

    in_specs = (P("grp", "mem", None, None, None), P(), P(), P(), P("grp", "mem"))
    out_specs = P(None, "mem", "grp")
    return jax.shard_map(body, mesh=mesh, in_specs=in_specs, out_specs=out_specs, check_vma=False)
```

```python
import functools
import math

import jax
import jax.numpy as jnp
from jax import lax
from jax.experimental import pallas as pl
from jax.experimental.pallas import tpu as pltpu
from jax.sharding import PartitionSpec as P

MESH = pl.DeviceIdType.MESH
TILE_ROWS = 8
LANES = 128
HALVES = 2
EARLY = 3
LAGS = (0, 2, 4, 4, 6, 8, 10)


def kernel(groups, members, coef_ref, group_ref, member_ref, active_ref, volume_ref, out_ref,
           vol, tloc, tin, col, rout, qout, inbox, aout, ain, own, fout, fin, tout, tpin, zout, zin,
           yout, yin, vol_sem, t_send, t_recv, c_send, r_send, q_send, m_recv, p_send, p_recv,
           a_send, a_recv, f_send, z_send, z_recv, y_send, y_recv):
    chunks, _, rows, width = tloc.shape
    stripes, samples, _, _, _ = vol.shape
    halves = chunks // stripes
    part = width // groups
    group_cols = part * halves
    chips = members // 2
    pairs = chips // 2
    g = lax.axis_index("grp")
    me = lax.axis_index("mem")
    chip = me // 2
    core = me % 2
    partner = me + 1 - 2 * core

    def bit(i):
        return (core + i) % 2

    def side(i):
        return (1 - bit(i)) * ((chip // 2) % 2) + bit(i) * (chip % 2)

    def mate(i):
        return chip + (1 - bit(i)) * (2 - 4 * ((chip // 2) % 2)) + bit(i) * (1 - 2 * (chip % 2))

    def pair_of(i):
        return (1 - bit(i)) * ((chip // 4) * 2 + chip % 2) + bit(i) * (chip // 2)

    def chip_of_pair(i, p, which):
        return (1 - bit(i)) * ((p // 2) * 4 + 2 * which + p % 2) + bit(i) * (2 * p + which)

    from_chip, from_pair = 3 * chips, 4 * chips
    sums_of_group = 3 * pairs
    factors_at = (groups - 1) * sums_of_group

    def fetch_first(d):
        return pltpu.make_async_copy(
            volume_ref.at[:, d, pl.ds(0, rows), :], vol.at[0, :, d], vol_sem.at[d])

    def fetch(j):
        start = pl.multiple_of(j * rows, TILE_ROWS)
        return pltpu.make_async_copy(
            volume_ref.at[:, :, pl.ds(start, rows), :], vol.at[j], vol_sem.at[members - 1 + j])

    def send(src, dst, send_sem, recv_sem, device):
        pltpu.make_async_remote_copy(
            src, dst, send_sem, recv_sem, device_id=device, device_id_type=MESH).start()

    def landed(ref, sem):
        pltpu.make_async_copy(ref, ref, sem).wait()

    def each(count, fn):
        def step(i, carry):
            fn(i)
            return carry
        lax.fori_loop(0, count, step, 0)

    barrier = pltpu.get_barrier_semaphore()
    each(members - 1, lambda off: pl.semaphore_signal(
        barrier, inc=1, device_id={"mem": (me + 1 + off) % members}, device_id_type=MESH))
    each(groups - 1, lambda off: pl.semaphore_signal(
        barrier, inc=1, device_id={"grp": (g + 1 + off) % groups}, device_id_type=MESH))

    each(members, lambda off: fetch_first((me + 1 + off) % members).start())
    each(stripes - 1, lambda j: fetch(j + 1).start())

    density_factor = math.sqrt(3.0 / (samples * groups * members) * math.log2(math.e))
    coef = [[coef_ref[c, p] * (0.5 if c < 3 else density_factor) for p in range(4)] for c in range(4)]
    active = active_ref[0, 0].astype(jnp.float32)
    half_active = active * 0.5
    ranks = [member_ref[g, i] for i in range(members)]
    near = [jnp.minimum(ranks[2 * q], ranks[2 * q + 1]) for q in range(chips)]
    far = [jnp.maximum(ranks[2 * q], ranks[2 * q + 1]) for q in range(chips)]
    orders = [group_ref[(g + groups - 1 - e) % groups] for e in range(groups)]

    def rank_of(member):
        return member_ref[g, member]

    def chip_rank(q):
        return jnp.minimum(rank_of(2 * q), rank_of(2 * q + 1))

    own_first = rank_of(me) < rank_of(partner)

    def march(i, d):
        j, h = i // halves, i % halves
        depth = jnp.zeros((TILE_ROWS, width), jnp.float32)
        light = jnp.ones((TILE_ROWS, width), jnp.float32)
        colour = [jnp.zeros((TILE_ROWS, width), jnp.float32) for _ in range(3)]
        starts = [pl.multiple_of(k * group_cols + h * part, LANES) for k in range(groups)]
        for k in range(samples):
            v = jnp.concatenate([vol[j, k, d, :, pl.ds(s, part)] for s in starts], axis=1)
            poly = [q[0] + v * (q[1] + v * (q[2] + v * q[3])) for q in coef]
            depth = depth - poly[3] * poly[3]
            after = jnp.exp2(depth)
            weight = light - after
            light = after
            colour = [colour[c] + weight * jnp.tanh(poly[c]) for c in range(3)]
        coverage = 1.0 - light
        tloc[i, d] = 1.0 - active * coverage
        for c in range(3):
            col[i, d, c] = half_active * (coverage + colour[c])

    early = min(EARLY, members)

    def prepare(i, off):
        d = (me + 1 + off) % members

        @pl.when(i == 0)
        def _():
            fetch_first(d).wait()
        march(i, d)

    def produce(i):
        @pl.when(jnp.logical_and(i > 0, i % halves == 0))
        def _():
            fetch(i // halves).wait()

        def unit(off):
            d = (me + 1 + off) % members

            @pl.when(jnp.logical_or(i > 0, off >= early))
            def _():
                prepare(i, off)

            @pl.when(off < members - 1)
            def _():
                send(tloc.at[i, d], tin.at[i, me], t_send, t_recv.at[i], {"mem": d})

            @pl.when(d % 2 != core)
            def _():
                send(col.at[i, d], inbox.at[i, pl.ds(3 * (d // 2), 3)], c_send, m_recv.at[i],
                     {"mem": partner})
        each(members, unit)
        tin[i, me] = tloc[i, me]

    def ratios(i):
        landed(tin.at[i, pl.ds(0, members - 1)], t_recv.at[i])
        t = [tin[i, m] for m in range(members)]

        def between(low, high):
            product = jnp.ones((TILE_ROWS, width), jnp.float32)
            for m in range(members):
                inside = ranks[m] < high
                if low is not None:
                    inside = jnp.logical_and(ranks[m] >= low, inside)
                product = product * jnp.where(inside, t[m], 1.0)
            return product

        def by_group(at, value):
            for k in range(groups):
                tout[i, k, at] = value[:, k * part:(k + 1) * part]

        for q in range(chips):
            rout[i, q] = between(near[q], far[q])

        def to_chip(off):
            k = (chip + 1 + off) % chips
            send(rout.at[i, k], inbox.at[i, from_chip + off], r_send, m_recv.at[i], {"mem": 2 * k + core})
        each(chips - 1, to_chip)

        total = t[0]
        for m in range(1, members):
            total = total * t[m]
        by_group(0, total)
        for p in range(pairs):
            a, b = chip_rank(chip_of_pair(i, p, 0)), chip_rank(chip_of_pair(i, p, 1))
            first, second = jnp.minimum(a, b), jnp.maximum(a, b)
            by_group(1 + p, between(None, first))
            qout[i, p] = between(first, second)
        my_pair = pair_of(i)

        def to_pair(off):
            p = (my_pair + 1 + off) % pairs
            send(qout.at[i, p], inbox.at[i, from_pair + off], q_send, m_recv.at[i],
                 {"mem": 2 * chip_of_pair(i, p, side(i)) + core})
        each(pairs - 1, to_pair)

        def to_group(off):
            k = (g + 1 + off) % groups
            send(tout.at[i, k], tpin.at[i, off], p_send, p_recv.at[i], {"grp": k})
        each(groups - 1, to_group)
        inbox[i, from_chip + chips - 1] = rout[i, chip]
        inbox[i, from_pair + pairs - 1] = qout[i, my_pair]
        tpin[i, groups - 1] = tout[i, g]

    def factors(i):
        landed(tpin.at[i, pl.ds(0, groups - 1)], p_recv.at[i])
        t = [tpin[i, e, 0] for e in range(groups)]
        total = t[0]
        for e in range(1, groups):
            total = total * t[e]
        row = pl.ds(pl.multiple_of((i // halves) * TILE_ROWS, TILE_ROWS), TILE_ROWS)
        column = pl.ds(pl.multiple_of((i % halves) * part, LANES), part)
        out_ref[3, row, column] = 1.0 - total
        for e in range(groups):
            before = jnp.ones_like(total)
            for o in range(groups):
                if o != e:
                    before = before * jnp.where(orders[o] < orders[e], t[o], 1.0)
            for p in range(pairs):
                fout[i, p, e] = before * tpin[i, e, 1 + p]
        my_pair = pair_of(i)

        def to_pair(off):
            p = (my_pair + 1 + off) % pairs
            send(fout.at[i, p], zin.at[i, pl.ds(factors_at + off * groups, groups)], f_send, z_recv.at[i],
                 {"mem": 2 * chip_of_pair(i, p, side(i)) + core})
        each(pairs - 1, to_pair)
        fin[i] = fout[i, my_pair]

    def chip_sums(i):
        landed(inbox.at[i, pl.ds(0, 4 * chips + pairs - 2)], m_recv.at[i])

        def sums(k, ref, p):
            ratio = inbox[i, from_chip + (chip - k - 1 + chips) % chips]
            own_factor = jnp.where(own_first, 1.0, ratio)
            other_factor = jnp.where(own_first, ratio, 1.0)
            for c in range(3):
                ref[i, p, c] = col[i, 2 * k + core, c] * own_factor + inbox[i, 3 * k + c] * other_factor
        each(pairs, lambda p: sums(chip_of_pair(i, p, 1 - side(i)), aout, p))
        send(aout.at[i], ain.at[i], a_send, a_recv.at[i], {"mem": 2 * mate(i) + core})
        each(pairs, lambda p: sums(chip_of_pair(i, p, side(i)), own, p))

    def pair_sums(i):
        landed(ain.at[i], a_recv.at[i])
        my_pair = pair_of(i)
        chip_first = chip_rank(chip) < chip_rank(mate(i))

        def unit(p):
            ratio = inbox[i, from_pair + (my_pair - p - 1 + pairs) % pairs]
            own_factor = jnp.where(chip_first, 1.0, ratio)
            other_factor = jnp.where(chip_first, ratio, 1.0)
            for c in range(3):
                total = own[i, p, c] * own_factor + ain[i, p, c] * other_factor
                for k in range(groups):
                    zout[i, k, 3 * p + c] = total[:, k * part:(k + 1) * part]
        each(pairs, unit)

        def to_group(off):
            k = (g + 1 + off) % groups
            send(zout.at[i, k], zin.at[i, pl.ds(off * sums_of_group, sums_of_group)], z_send, z_recv.at[i],
                 {"grp": k})
        each(groups - 1, to_group)

    def combine(i):
        landed(zin.at[i, pl.ds(0, factors_at + (pairs - 1) * groups)], z_recv.at[i])
        my_pair = pair_of(i)

        def sums(p, factor, ref, at):
            for c in range(3):
                total = factor(groups - 1) * zout[i, g, 3 * p + c]
                for e in range(groups - 1):
                    total = total + factor(e) * zin[i, e * sums_of_group + 3 * p + c]
                ref[i, at, c] = total

        def unit(off):
            p = (my_pair + 1 + off) % pairs
            back = (my_pair - p - 1 + pairs) % pairs
            sums(p, lambda e: zin[i, factors_at + back * groups + e], yout, p)
            send(yout.at[i, p], yin.at[i, off], y_send, y_recv.at[i],
                 {"mem": 2 * chip_of_pair(i, p, side(i)) + core})
        each(pairs - 1, unit)
        sums(my_pair, lambda e: fin[i, e], yin, pairs - 1)

    def finish(i):
        if pairs > 1:
            landed(yin.at[i, pl.ds(0, pairs - 1)], y_recv.at[i])
        row = pl.ds(pl.multiple_of((i // halves) * TILE_ROWS, TILE_ROWS), TILE_ROWS)
        column = pl.ds(pl.multiple_of((i % halves) * part, LANES), part)
        for c in range(3):
            colour = yin[i, 0, c]
            for p in range(1, pairs):
                colour = colour + yin[i, p, c]
            out_ref[c, row, column] = colour

    stages = (produce, ratios, factors, chip_sums, pair_sums, combine, finish)

    def step(s):
        for lag, stage in zip(LAGS, stages):
            @pl.when(jnp.logical_and(s >= lag, s < chunks + lag))
            def _():
                stage(s - lag)

    each(early, lambda off: prepare(0, off))
    pl.semaphore_wait(barrier, members + groups - 2)
    each(chunks + LAGS[-1], step)

    landed(tloc.at[:, pl.ds(0, members - 1)], t_send)
    landed(inbox.at[:, pl.ds(0, 3 * chips)], c_send)
    landed(rout.at[:, pl.ds(0, chips - 1)], r_send)
    landed(tout.at[:, pl.ds(0, groups - 1)], p_send)
    landed(aout, a_send)
    landed(zout.at[:, pl.ds(0, groups - 1)], z_send)
    if pairs > 1:
        landed(qout.at[:, pl.ds(0, pairs - 1)], q_send)
        landed(fout.at[:, pl.ds(0, pairs - 1)], f_send)
        landed(yout.at[:, pl.ds(0, pairs - 1)], y_send)


def solution(mesh):
    groups, members = mesh.shape["grp"], mesh.shape["mem"]
    chips = members // 2
    pairs = chips // 2

    def body(volume, transfer_coef, group_order, member_order, active_mask):
        samples, image_rows, cols = volume.shape[2:]
        block_rows = image_rows // members
        stripes = block_rows // TILE_ROWS
        group_cols = cols // groups
        halves = min(HALVES, group_cols // LANES)
        part = group_cols // halves
        chunks = stripes * halves
        smem = pl.BlockSpec(memory_space=pltpu.SMEM)
        dma = pltpu.SemaphoreType.DMA

        def vmem(*shape):
            return pltpu.VMEM(shape, jnp.float32)

        tile = (TILE_ROWS, part * groups)
        piece = (TILE_ROWS, part)
        scratch = [
            vmem(stripes, samples, members, TILE_ROWS, cols),
            vmem(chunks, members, *tile),
            vmem(chunks, members, *tile),
            vmem(chunks, members, 3, *tile),
            vmem(chunks, chips, *tile),
            vmem(chunks, pairs, *tile),
            vmem(chunks, 4 * chips + pairs, *tile),
            vmem(chunks, pairs, 3, *tile),
            vmem(chunks, pairs, 3, *tile),
            vmem(chunks, pairs, 3, *tile),
            vmem(chunks, pairs, groups, *piece),
            vmem(chunks, groups, *piece),
            vmem(chunks, groups, 1 + pairs, *piece),
            vmem(chunks, groups, 1 + pairs, *piece),
            vmem(chunks, groups, 3 * pairs, *piece),
            vmem(chunks, (groups - 1) * 3 * pairs + (pairs - 1) * groups, *piece),
            vmem(chunks, pairs, 3, *piece),
            vmem(chunks, pairs, 3, *piece),
            dma((stripes + members - 1,)),
            dma, dma((chunks,)),
            dma, dma, dma, dma((chunks,)),
            dma, dma((chunks,)),
            dma, dma((chunks,)),
            dma, dma, dma((chunks,)),
            dma, dma((chunks,)),
        ]
        return pl.pallas_call(
            functools.partial(kernel, groups, members),
            out_shape=pltpu.VMEM((4, block_rows, group_cols), jnp.float32),
            in_specs=[smem, smem, smem, smem, pl.BlockSpec(memory_space=pl.ANY)],
            out_specs=pl.BlockSpec(memory_space=pltpu.VMEM),
            scratch_shapes=scratch,
            compiler_params=pltpu.CompilerParams(
                collective_id=0, has_side_effects=True, vmem_limit_bytes=60 * 1024 * 1024),
        )(transfer_coef, group_order, member_order, active_mask,
          volume.reshape(samples, members, block_rows, cols))

    in_specs = (P("grp", "mem", None, None, None), P(), P(), P(), P("grp", "mem"))
    out_specs = P(None, "mem", "grp")
    return jax.shard_map(body, mesh=mesh, in_specs=in_specs, out_specs=out_specs, check_vma=False)
```

```python
import functools
import math

import jax
import jax.numpy as jnp
from jax import lax
from jax.experimental import pallas as pl
from jax.experimental.pallas import tpu as pltpu
from jax.sharding import PartitionSpec as P

MESH = pl.DeviceIdType.MESH
TILE_ROWS = 8
LANES = 128
HALVES = 2
EARLY = 3
LAGS = (0, 2, 16, 4, 6, 26, 38)


def kernel(groups, members, coef_ref, group_ref, member_ref, active_ref, volume_ref, out_ref,
           vol, tloc, tin, col, rout, qout, inbox, aout, ain, own, tfirst, fout, fin, tout, tpin, zout, zin,
           yout, last, vol_sem, t_send, t_recv, c_send, r_send, q_send, m_recv, p_send, p_recv,
           a_send, f_send, z_send, z_recv, y_send, l_recv):
    chunks, _, rows, width = tloc.shape
    stripes, samples, _, _, _ = vol.shape
    halves = chunks // stripes
    part = width // groups
    group_cols = part * halves
    chips = members // 2
    pairs = chips // 2
    g = lax.axis_index("grp")
    me = lax.axis_index("mem")
    chip = me // 2
    core = me % 2
    partner = me + 1 - 2 * core

    def bit(i):
        return (core + i) % 2

    def side(i):
        return (1 - bit(i)) * ((chip // 2) % 2) + bit(i) * (chip % 2)

    def mate(i):
        return chip + (1 - bit(i)) * (2 - 4 * ((chip // 2) % 2)) + bit(i) * (1 - 2 * (chip % 2))

    def pair_of(i):
        return (1 - bit(i)) * ((chip // 4) * 2 + chip % 2) + bit(i) * (chip // 2)

    def chip_of_pair(i, p, which):
        return (1 - bit(i)) * ((p // 2) * 4 + 2 * which + p % 2) + bit(i) * (2 * p + which)

    from_chip, from_pair = 3 * chips, 4 * chips
    sums_of_group = 3 * (pairs - 1)
    factors_at = (groups - 1) * sums_of_group
    colours_at = (groups - 1) * 3
    low_half = 1 - g // (groups // 2)

    def far_first(n):
        return low_half * (groups - 2 - n) + (1 - low_half) * n

    def fetch_first(d):
        return pltpu.make_async_copy(
            volume_ref.at[:, d, pl.ds(0, rows), :], vol.at[0, :, d], vol_sem.at[d])

    def fetch(j):
        start = pl.multiple_of(j * rows, TILE_ROWS)
        return pltpu.make_async_copy(
            volume_ref.at[:, :, pl.ds(start, rows), :], vol.at[j], vol_sem.at[members - 1 + j])

    def send(src, dst, send_sem, recv_sem, device):
        pltpu.make_async_remote_copy(
            src, dst, send_sem, recv_sem, device_id=device, device_id_type=MESH).start()

    def landed(ref, sem):
        pltpu.make_async_copy(ref, ref, sem).wait()

    def each(count, fn):
        def step(i, carry):
            fn(i)
            return carry
        lax.fori_loop(0, count, step, 0)

    barrier = pltpu.get_barrier_semaphore()
    each(members - 1, lambda off: pl.semaphore_signal(
        barrier, inc=1, device_id={"mem": (me + 1 + off) % members}, device_id_type=MESH))
    each(groups - 1, lambda off: pl.semaphore_signal(
        barrier, inc=1, device_id={"grp": (g + 1 + off) % groups}, device_id_type=MESH))

    each(members, lambda off: fetch_first((me + 1 + off) % members).start())
    each(stripes - 1, lambda j: fetch(j + 1).start())

    density_factor = math.sqrt(3.0 / (samples * groups * members) * math.log2(math.e))
    coef = [[coef_ref[c, p] * (0.5 if c < 3 else density_factor) for p in range(4)] for c in range(4)]
    active = active_ref[0, 0].astype(jnp.float32)
    half_active = active * 0.5
    ranks = [member_ref[g, i] for i in range(members)]
    near = [jnp.minimum(ranks[2 * q], ranks[2 * q + 1]) for q in range(chips)]
    far = [jnp.maximum(ranks[2 * q], ranks[2 * q + 1]) for q in range(chips)]
    orders = [group_ref[(g + groups - 1 - e) % groups] for e in range(groups)]

    def rank_of(member):
        return member_ref[g, member]

    def chip_rank(q):
        return jnp.minimum(rank_of(2 * q), rank_of(2 * q + 1))

    own_first = rank_of(me) < rank_of(partner)

    def march(i, d):
        j, h = i // halves, i % halves
        depth = jnp.zeros((TILE_ROWS, width), jnp.float32)
        light = jnp.ones((TILE_ROWS, width), jnp.float32)
        colour = [jnp.zeros((TILE_ROWS, width), jnp.float32) for _ in range(3)]
        starts = [pl.multiple_of(k * group_cols + h * part, LANES) for k in range(groups)]
        for k in range(samples):
            v = jnp.concatenate([vol[j, k, d, :, pl.ds(s, part)] for s in starts], axis=1)
            poly = [q[0] + v * (q[1] + v * (q[2] + v * q[3])) for q in coef]
            depth = depth - poly[3] * poly[3]
            after = jnp.exp2(depth)
            weight = light - after
            light = after
            colour = [colour[c] + weight * jnp.tanh(poly[c]) for c in range(3)]
        coverage = 1.0 - light
        tloc[i, d] = 1.0 - active * coverage
        for c in range(3):
            col[i, d, c] = half_active * (coverage + colour[c])

    early = min(EARLY, members)

    def prepare(i, off):
        d = (me + 1 + off) % members

        @pl.when(i == 0)
        def _():
            fetch_first(d).wait()
        march(i, d)

    def produce(i):
        @pl.when(jnp.logical_and(i > 0, i % halves == 0))
        def _():
            fetch(i // halves).wait()

        def unit(off):
            d = (me + 1 + off) % members

            @pl.when(jnp.logical_or(i > 0, off >= early))
            def _():
                prepare(i, off)

            @pl.when(off < members - 1)
            def _():
                send(tloc.at[i, d], tin.at[i, me], t_send, t_recv.at[i], {"mem": d})

            @pl.when(d % 2 != core)
            def _():
                send(col.at[i, d], inbox.at[i, pl.ds(3 * (d // 2), 3)], c_send, m_recv.at[i],
                     {"mem": partner})
        each(members, unit)
        tin[i, me] = tloc[i, me]

    def ratios(i):
        landed(tin.at[i, pl.ds(0, members - 1)], t_recv.at[i])
        t = [tin[i, m] for m in range(members)]

        def between(low, high):
            product = jnp.ones((TILE_ROWS, width), jnp.float32)
            for m in range(members):
                inside = ranks[m] < high
                if low is not None:
                    inside = jnp.logical_and(ranks[m] >= low, inside)
                product = product * jnp.where(inside, t[m], 1.0)
            return product

        def by_group(at, value):
            for k in range(groups):
                tout[i, k, at] = value[:, k * part:(k + 1) * part]

        for q in range(chips):
            rout[i, q] = between(near[q], far[q])

        def to_chip(off):
            k = (chip + 1 + off) % chips
            send(rout.at[i, k], inbox.at[i, from_chip + off], r_send, m_recv.at[i], {"mem": 2 * k + core})
        each(chips - 1, to_chip)

        total = t[0]
        for m in range(1, members):
            total = total * t[m]
        by_group(0, total)
        my_pair = pair_of(i)
        for off in range(pairs):
            p = (my_pair + 1 + off) % pairs
            a, b = chip_rank(chip_of_pair(i, p, 0)), chip_rank(chip_of_pair(i, p, 1))
            first, second = jnp.minimum(a, b), jnp.maximum(a, b)
            ahead = between(None, first)
            if off < pairs - 1:
                qout[i, off] = between(first, second)
                by_group(1 + off, ahead)
            else:
                inbox[i, from_pair + off] = between(first, second)
                tfirst[i] = ahead

        def to_pair(off):
            p = (my_pair + 1 + off) % pairs
            send(qout.at[i, off], inbox.at[i, from_pair + off], q_send, m_recv.at[i],
                 {"mem": 2 * chip_of_pair(i, p, side(i)) + core})
        each(pairs - 1, to_pair)

        def to_group(n):
            off = far_first(n)
            k = (g + 1 + off) % groups
            send(tout.at[i, k], tpin.at[i, off], p_send, p_recv.at[i], {"grp": k})
        each(groups - 1, to_group)
        inbox[i, from_chip + chips - 1] = rout[i, chip]
        tpin[i, groups - 1] = tout[i, g]

    def factors(i):
        landed(tpin.at[i, pl.ds(0, groups - 1)], p_recv.at[i])
        t = [tpin[i, e, 0] for e in range(groups)]
        total = t[0]
        for e in range(1, groups):
            total = total * t[e]
        row = pl.ds(pl.multiple_of((i // halves) * TILE_ROWS, TILE_ROWS), TILE_ROWS)
        column = pl.ds(pl.multiple_of((i % halves) * part, LANES), part)
        out_ref[3, row, column] = 1.0 - total
        for e in range(groups):
            before = jnp.ones_like(total)
            for o in range(groups):
                if o != e:
                    before = before * jnp.where(orders[o] < orders[e], t[o], 1.0)
            fin[i, e] = before
            for off in range(pairs - 1):
                fout[i, off, e] = before * tpin[i, e, 1 + off]
        my_pair = pair_of(i)

        def to_pair(off):
            p = (my_pair + 1 + off) % pairs
            send(fout.at[i, off], zin.at[i, pl.ds(factors_at + off * groups, groups)], f_send, z_recv.at[i],
                 {"mem": 2 * chip_of_pair(i, p, side(i)) + core})
        each(pairs - 1, to_pair)

    def chip_sums(i):
        landed(inbox.at[i, pl.ds(0, 4 * chips + pairs - 2)], m_recv.at[i])

        def sums(k, ref, p):
            ratio = inbox[i, from_chip + (chip - k - 1 + chips) % chips]
            own_factor = jnp.where(own_first, 1.0, ratio)
            other_factor = jnp.where(own_first, ratio, 1.0)
            for c in range(3):
                ref[i, p, c] = col[i, 2 * k + core, c] * own_factor + inbox[i, 3 * k + c] * other_factor
        each(pairs, lambda p: sums(chip_of_pair(i, p, 1 - side(i)), aout, p))
        send(aout.at[i], ain.at[i], a_send, t_recv.at[i], {"mem": 2 * mate(i) + core})
        each(pairs, lambda p: sums(chip_of_pair(i, p, side(i)), own, p))

    def pair_sums(i):
        landed(ain.at[i], t_recv.at[i])
        my_pair = pair_of(i)
        chip_first = chip_rank(chip) < chip_rank(mate(i))

        def sums(off, scale):
            p = (my_pair + 1 + off) % pairs
            ratio = inbox[i, from_pair + (pairs - 2 - off) % pairs]
            own_factor = jnp.where(chip_first, 1.0, ratio)
            other_factor = jnp.where(chip_first, ratio, 1.0)
            for c in range(3):
                total = own[i, p, c] * own_factor + ain[i, p, c] * other_factor
                if scale is not None:
                    total = total * scale
                for k in range(groups):
                    zout[i, k, 3 * off + c] = total[:, k * part:(k + 1) * part]

        for off in range(pairs - 1):
            sums(off, None)

        def others_to_group(n):
            off = far_first(n)
            k = (g + 1 + off) % groups
            send(zout.at[i, k, pl.ds(0, sums_of_group)],
                 zin.at[i, pl.ds(off * sums_of_group, sums_of_group)], z_send, z_recv.at[i], {"grp": k})
        each(groups - 1, others_to_group)
        sums(pairs - 1, tfirst[i])

        def own_to_group(n):
            off = far_first(n)
            k = (g + 1 + off) % groups
            send(zout.at[i, k, pl.ds(sums_of_group, 3)], last.at[i, pl.ds(off * 3, 3)],
                 z_send, l_recv.at[i], {"grp": k})
        each(groups - 1, own_to_group)

    def combine(i):
        landed(zin.at[i, pl.ds(0, factors_at + (pairs - 1) * groups)], z_recv.at[i])
        my_pair = pair_of(i)

        for off in range(pairs - 1):
            p = (my_pair + 1 + off) % pairs
            back = factors_at + (pairs - 2 - off) * groups
            for c in range(3):
                total = zin[i, back + groups - 1] * zout[i, g, 3 * off + c]
                for e in range(groups - 1):
                    total = total + zin[i, back + e] * zin[i, e * sums_of_group + 3 * off + c]
                yout[i, off, c] = total
            send(yout.at[i, off], last.at[i, pl.ds(colours_at + 3 * off, 3)], y_send, l_recv.at[i],
                 {"mem": 2 * chip_of_pair(i, p, side(i)) + core})

    def finish(i):
        landed(last.at[i, pl.ds(0, colours_at + sums_of_group)], l_recv.at[i])
        row = pl.ds(pl.multiple_of((i // halves) * TILE_ROWS, TILE_ROWS), TILE_ROWS)
        column = pl.ds(pl.multiple_of((i % halves) * part, LANES), part)
        for c in range(3):
            colour = fin[i, groups - 1] * zout[i, g, sums_of_group + c]
            for e in range(groups - 1):
                colour = colour + fin[i, e] * last[i, e * 3 + c]
            for off in range(pairs - 1):
                colour = colour + last[i, colours_at + 3 * off + c]
            out_ref[c, row, column] = colour

    stages = (produce, ratios, factors, chip_sums, pair_sums, combine, finish)

    def step(s):
        for lag, stage in zip(LAGS, stages):
            @pl.when(jnp.logical_and(s >= lag, s < chunks + lag))
            def _():
                stage(s - lag)

    each(early, lambda off: prepare(0, off))
    pl.semaphore_wait(barrier, members + groups - 2)
    each(chunks + LAGS[-1], step)

    landed(tloc.at[:, pl.ds(0, members - 1)], t_send)
    landed(inbox.at[:, pl.ds(0, 3 * chips)], c_send)
    landed(rout.at[:, pl.ds(0, chips - 1)], r_send)
    landed(tout.at[:, pl.ds(0, groups - 1)], p_send)
    landed(aout, a_send)
    landed(zout.at[:, pl.ds(0, groups - 1)], z_send)
    landed(qout, q_send)
    landed(fout, f_send)
    landed(yout, y_send)


def solution(mesh):
    groups, members = mesh.shape["grp"], mesh.shape["mem"]
    chips = members // 2
    pairs = chips // 2

    def body(volume, transfer_coef, group_order, member_order, active_mask):
        samples, image_rows, cols = volume.shape[2:]
        block_rows = image_rows // members
        stripes = block_rows // TILE_ROWS
        group_cols = cols // groups
        halves = min(HALVES, group_cols // LANES)
        part = group_cols // halves
        chunks = stripes * halves
        smem = pl.BlockSpec(memory_space=pltpu.SMEM)
        dma = pltpu.SemaphoreType.DMA

        def vmem(*shape):
            return pltpu.VMEM(shape, jnp.float32)

        tile = (TILE_ROWS, part * groups)
        piece = (TILE_ROWS, part)
        scratch = [
            vmem(stripes, samples, members, TILE_ROWS, cols),
            vmem(chunks, members, *tile),
            vmem(chunks, members, *tile),
            vmem(chunks, members, 3, *tile),
            vmem(chunks, chips, *tile),
            vmem(chunks, pairs - 1, *tile),
            vmem(chunks, 4 * chips + pairs, *tile),
            vmem(chunks, pairs, 3, *tile),
            vmem(chunks, pairs, 3, *tile),
            vmem(chunks, pairs, 3, *tile),
            vmem(chunks, *tile),
            vmem(chunks, pairs - 1, groups, *piece),
            vmem(chunks, groups, *piece),
            vmem(chunks, groups, pairs, *piece),
            vmem(chunks, groups, pairs, *piece),
            vmem(chunks, groups, 3 * pairs, *piece),
            vmem(chunks, (groups - 1) * 3 * (pairs - 1) + (pairs - 1) * groups, *piece),
            vmem(chunks, pairs - 1, 3, *piece),
            vmem(chunks, (groups - 1) * 3 + 3 * (pairs - 1), *piece),
            dma((stripes + members - 1,)),
            dma, dma((chunks,)),
            dma, dma, dma, dma((chunks,)),
            dma, dma((chunks,)),
            dma,
            dma, dma, dma((chunks,)),
            dma, dma((chunks,)),
        ]
        return pl.pallas_call(
            functools.partial(kernel, groups, members),
            out_shape=pltpu.VMEM((4, block_rows, group_cols), jnp.float32),
            in_specs=[smem, smem, smem, smem, pl.BlockSpec(memory_space=pl.ANY)],
            out_specs=pl.BlockSpec(memory_space=pltpu.VMEM),
            scratch_shapes=scratch,
            compiler_params=pltpu.CompilerParams(
                collective_id=0, has_side_effects=True, vmem_limit_bytes=60 * 1024 * 1024),
        )(transfer_coef, group_order, member_order, active_mask,
          volume.reshape(samples, members, block_rows, cols))

    in_specs = (P("grp", "mem", None, None, None), P(), P(), P(), P("grp", "mem"))
    out_specs = P(None, "mem", "grp")
    return jax.shard_map(body, mesh=mesh, in_specs=in_specs, out_specs=out_specs, check_vma=False)
```

```python
import functools
import math

import jax
import jax.numpy as jnp
from jax import lax
from jax.experimental import pallas as pl
from jax.experimental.pallas import tpu as pltpu
from jax.sharding import PartitionSpec as P

MESH = pl.DeviceIdType.MESH
TILE_ROWS = 8
LANES = 128
HALVES = 2
EARLY = 3
LAGS = (0, 2, 16, 4, 6, 26, 38)


def kernel(groups, members, coef_ref, group_ref, member_ref, active_ref, volume_ref, out_ref,
           vol, tloc, tin, col, rout, qout, inbox, aout, ain, own, tfirst, fout, fin, tout, tpin, zout, zin,
           yout, last, vol_sem, t_send, t_recv, c_send, r_send, q_send, m_recv, p_send, p_recv,
           a_send, f_send, z_send, z_recv, y_send, l_recv):
    chunks, _, rows, width = tloc.shape
    stripes, samples, _, _, _ = vol.shape
    halves = chunks // stripes
    group_of = chunks // 2
    part = width // groups
    group_cols = part * halves
    chips = members // 2
    pairs = chips // 2
    g = lax.axis_index("grp")
    me = lax.axis_index("mem")
    chip = me // 2
    core = me % 2
    partner = me + 1 - 2 * core

    def bit(i):
        return (core + i) % 2

    def side(i):
        return (1 - bit(i)) * ((chip // 2) % 2) + bit(i) * (chip % 2)

    def mate(i):
        return chip + (1 - bit(i)) * (2 - 4 * ((chip // 2) % 2)) + bit(i) * (1 - 2 * (chip % 2))

    def pair_of(i):
        return (1 - bit(i)) * ((chip // 4) * 2 + chip % 2) + bit(i) * (chip // 2)

    def chip_of_pair(i, p, which):
        return (1 - bit(i)) * ((p // 2) * 4 + 2 * which + p % 2) + bit(i) * (2 * p + which)

    from_chip, from_pair = 3 * chips, 4 * chips
    sums_of_group = 3 * (pairs - 1)
    factors_at = (groups - 1) * sums_of_group
    colours_at = (groups - 1) * 3
    low_half = 1 - g // (groups // 2)

    def far_first(n):
        return low_half * (groups - 2 - n) + (1 - low_half) * n

    def fetch_first(d):
        return pltpu.make_async_copy(
            volume_ref.at[:, d, pl.ds(0, rows), :], vol.at[0, :, d], vol_sem.at[d])

    def fetch(j):
        start = pl.multiple_of(j * rows, TILE_ROWS)
        return pltpu.make_async_copy(
            volume_ref.at[:, :, pl.ds(start, rows), :], vol.at[j], vol_sem.at[members - 1 + j])

    def send(src, dst, send_sem, recv_sem, device):
        pltpu.make_async_remote_copy(
            src, dst, send_sem, recv_sem, device_id=device, device_id_type=MESH).start()

    def landed(ref, sem):
        pltpu.make_async_copy(ref, ref, sem).wait()

    def each(count, fn):
        def step(i, carry):
            fn(i)
            return carry
        lax.fori_loop(0, count, step, 0)

    barrier = pltpu.get_barrier_semaphore()
    each(members - 1, lambda off: pl.semaphore_signal(
        barrier, inc=1, device_id={"mem": (me + 1 + off) % members}, device_id_type=MESH))
    each(groups - 1, lambda off: pl.semaphore_signal(
        barrier, inc=1, device_id={"grp": (g + 1 + off) % groups}, device_id_type=MESH))

    each(members, lambda off: fetch_first((me + 1 + off) % members).start())
    each(stripes - 1, lambda j: fetch(j + 1).start())

    density_factor = math.sqrt(3.0 / (samples * groups * members) * math.log2(math.e))
    coef = [[coef_ref[c, p] * (0.5 if c < 3 else density_factor) for p in range(4)] for c in range(4)]
    active = active_ref[0, 0].astype(jnp.float32)
    half_active = active * 0.5
    ranks = [member_ref[g, i] for i in range(members)]
    near = [jnp.minimum(ranks[2 * q], ranks[2 * q + 1]) for q in range(chips)]
    far = [jnp.maximum(ranks[2 * q], ranks[2 * q + 1]) for q in range(chips)]
    orders = [group_ref[(g + groups - 1 - e) % groups] for e in range(groups)]

    def rank_of(member):
        return member_ref[g, member]

    def chip_rank(q):
        return jnp.minimum(rank_of(2 * q), rank_of(2 * q + 1))

    own_first = rank_of(me) < rank_of(partner)

    def march(i, d):
        j, h = i // halves, i % halves
        depth = jnp.zeros((TILE_ROWS, width), jnp.float32)
        light = jnp.ones((TILE_ROWS, width), jnp.float32)
        colour = [jnp.zeros((TILE_ROWS, width), jnp.float32) for _ in range(3)]
        starts = [pl.multiple_of(k * group_cols + h * part, LANES) for k in range(groups)]
        for k in range(samples):
            v = jnp.concatenate([vol[j, k, d, :, pl.ds(s, part)] for s in starts], axis=1)
            poly = [q[0] + v * (q[1] + v * (q[2] + v * q[3])) for q in coef]
            depth = depth - poly[3] * poly[3]
            after = jnp.exp2(depth)
            weight = light - after
            light = after
            colour = [colour[c] + weight * jnp.tanh(poly[c]) for c in range(3)]
        coverage = 1.0 - light
        tloc[i, d] = 1.0 - active * coverage
        for c in range(3):
            col[i, d, c] = half_active * (coverage + colour[c])

    early = min(EARLY, members)

    def prepare(i, off):
        d = (me + 1 + off) % members

        @pl.when(i == 0)
        def _():
            fetch_first(d).wait()
        march(i, d)

    def produce(i):
        @pl.when(jnp.logical_and(i > 0, i % halves == 0))
        def _():
            fetch(i // halves).wait()

        def unit(off):
            d = (me + 1 + off) % members

            @pl.when(jnp.logical_or(i > 0, off >= early))
            def _():
                prepare(i, off)

            @pl.when(off < members - 1)
            def _():
                send(tloc.at[i, d], tin.at[i, me], t_send, t_recv.at[i], {"mem": d})

            @pl.when(d % 2 != core)
            def _():
                send(col.at[i, d], inbox.at[i, pl.ds(3 * (d // 2), 3)], c_send, m_recv.at[i],
                     {"mem": partner})
        each(members, unit)
        tin[i, me] = tloc[i, me]

    def ratios(i):
        landed(tin.at[i, pl.ds(0, members - 1)], t_recv.at[i])
        t = [tin[i, m] for m in range(members)]

        def between(low, high):
            product = jnp.ones((TILE_ROWS, width), jnp.float32)
            for m in range(members):
                inside = ranks[m] < high
                if low is not None:
                    inside = jnp.logical_and(ranks[m] >= low, inside)
                product = product * jnp.where(inside, t[m], 1.0)
            return product

        def by_group(at, value):
            for k in range(groups):
                tout[i, k, at] = value[:, k * part:(k + 1) * part]

        for q in range(chips):
            rout[i, q] = between(near[q], far[q])

        def to_chip(off):
            k = (chip + 1 + off) % chips
            send(rout.at[i, k], inbox.at[i, from_chip + off], r_send, m_recv.at[i], {"mem": 2 * k + core})
        each(chips - 1, to_chip)

        total = t[0]
        for m in range(1, members):
            total = total * t[m]
        by_group(0, total)
        my_pair = pair_of(i)
        for off in range(pairs):
            p = (my_pair + 1 + off) % pairs
            a, b = chip_rank(chip_of_pair(i, p, 0)), chip_rank(chip_of_pair(i, p, 1))
            first, second = jnp.minimum(a, b), jnp.maximum(a, b)
            ahead = between(None, first)
            if off < pairs - 1:
                qout[i, off] = between(first, second)
                by_group(1 + off, ahead)
            else:
                inbox[i, from_pair + off] = between(first, second)
                tfirst[i] = ahead

        def to_pair(off):
            p = (my_pair + 1 + off) % pairs
            send(qout.at[i, off], inbox.at[i, from_pair + off], q_send, m_recv.at[i],
                 {"mem": 2 * chip_of_pair(i, p, side(i)) + core})
        each(pairs - 1, to_pair)

        def to_group(n):
            off = far_first(n)
            k = (g + 1 + off) % groups
            send(tout.at[i, k], tpin.at[i, off], p_send, p_recv.at[i // group_of], {"grp": k})
        each(groups - 1, to_group)
        inbox[i, from_chip + chips - 1] = rout[i, chip]
        tpin[i, groups - 1] = tout[i, g]

    def factors(i):
        @pl.when(i % group_of == 0)
        def _():
            landed(tpin.at[pl.ds(i, group_of), pl.ds(0, groups - 1)], p_recv.at[i // group_of])

        t = [tpin[i, e, 0] for e in range(groups)]
        total = t[0]
        for e in range(1, groups):
            total = total * t[e]
        row = pl.ds(pl.multiple_of((i // halves) * TILE_ROWS, TILE_ROWS), TILE_ROWS)
        column = pl.ds(pl.multiple_of((i % halves) * part, LANES), part)
        out_ref[3, row, column] = 1.0 - total
        for e in range(groups):
            before = jnp.ones_like(total)
            for o in range(groups):
                if o != e:
                    before = before * jnp.where(orders[o] < orders[e], t[o], 1.0)
            fin[i, e] = before
            for off in range(pairs - 1):
                fout[i, off, e] = before * tpin[i, e, 1 + off]
        my_pair = pair_of(i)

        def to_pair(off):
            p = (my_pair + 1 + off) % pairs
            send(fout.at[i, off], zin.at[i, pl.ds(factors_at + off * groups, groups)], f_send, z_recv.at[i],
                 {"mem": 2 * chip_of_pair(i, p, side(i)) + core})
        each(pairs - 1, to_pair)

    def chip_sums(i):
        landed(inbox.at[i, pl.ds(0, 4 * chips + pairs - 2)], m_recv.at[i])

        def sums(k, ref, p):
            ratio = inbox[i, from_chip + (chip - k - 1 + chips) % chips]
            own_factor = jnp.where(own_first, 1.0, ratio)
            other_factor = jnp.where(own_first, ratio, 1.0)
            for c in range(3):
                ref[i, p, c] = col[i, 2 * k + core, c] * own_factor + inbox[i, 3 * k + c] * other_factor
        each(pairs, lambda p: sums(chip_of_pair(i, p, 1 - side(i)), aout, p))
        send(aout.at[i], ain.at[i], a_send, t_recv.at[i], {"mem": 2 * mate(i) + core})
        each(pairs, lambda p: sums(chip_of_pair(i, p, side(i)), own, p))

    def pair_sums(i):
        landed(ain.at[i], t_recv.at[i])
        my_pair = pair_of(i)
        chip_first = chip_rank(chip) < chip_rank(mate(i))

        def sums(off, scale):
            p = (my_pair + 1 + off) % pairs
            ratio = inbox[i, from_pair + (pairs - 2 - off) % pairs]
            own_factor = jnp.where(chip_first, 1.0, ratio)
            other_factor = jnp.where(chip_first, ratio, 1.0)
            for c in range(3):
                total = own[i, p, c] * own_factor + ain[i, p, c] * other_factor
                if scale is not None:
                    total = total * scale
                for k in range(groups):
                    zout[i, k, 3 * off + c] = total[:, k * part:(k + 1) * part]

        for off in range(pairs - 1):
            sums(off, None)

        def others_to_group(n):
            off = far_first(n)
            k = (g + 1 + off) % groups
            send(zout.at[i, k, pl.ds(0, sums_of_group)],
                 zin.at[i, pl.ds(off * sums_of_group, sums_of_group)], z_send, z_recv.at[i], {"grp": k})
        each(groups - 1, others_to_group)
        sums(pairs - 1, tfirst[i])

        def own_to_group(n):
            off = far_first(n)
            k = (g + 1 + off) % groups
            send(zout.at[i, k, pl.ds(sums_of_group, 3)], last.at[i, pl.ds(off * 3, 3)],
                 z_send, l_recv.at[i], {"grp": k})
        each(groups - 1, own_to_group)

    def combine(i):
        landed(zin.at[i, pl.ds(0, factors_at + (pairs - 1) * groups)], z_recv.at[i])
        my_pair = pair_of(i)

        for off in range(pairs - 1):
            p = (my_pair + 1 + off) % pairs
            back = factors_at + (pairs - 2 - off) * groups
            for c in range(3):
                total = zin[i, back + groups - 1] * zout[i, g, 3 * off + c]
                for e in range(groups - 1):
                    total = total + zin[i, back + e] * zin[i, e * sums_of_group + 3 * off + c]
                yout[i, off, c] = total
            send(yout.at[i, off], last.at[i, pl.ds(colours_at + 3 * off, 3)], y_send, l_recv.at[i],
                 {"mem": 2 * chip_of_pair(i, p, side(i)) + core})

    def finish(i):
        landed(last.at[i, pl.ds(0, colours_at + sums_of_group)], l_recv.at[i])
        row = pl.ds(pl.multiple_of((i // halves) * TILE_ROWS, TILE_ROWS), TILE_ROWS)
        column = pl.ds(pl.multiple_of((i % halves) * part, LANES), part)
        for c in range(3):
            colour = fin[i, groups - 1] * zout[i, g, sums_of_group + c]
            for e in range(groups - 1):
                colour = colour + fin[i, e] * last[i, e * 3 + c]
            for off in range(pairs - 1):
                colour = colour + last[i, colours_at + 3 * off + c]
            out_ref[c, row, column] = colour

    stages = (produce, ratios, factors, chip_sums, pair_sums, combine, finish)

    def step(s):
        for lag, stage in zip(LAGS, stages):
            @pl.when(jnp.logical_and(s >= lag, s < chunks + lag))
            def _():
                stage(s - lag)

    each(early, lambda off: prepare(0, off))
    pl.semaphore_wait(barrier, members + groups - 2)
    each(chunks + LAGS[-1], step)

    landed(tloc.at[:, pl.ds(0, members - 1)], t_send)
    landed(inbox.at[:, pl.ds(0, 3 * chips)], c_send)
    landed(rout.at[:, pl.ds(0, chips - 1)], r_send)
    landed(tout.at[:, pl.ds(0, groups - 1)], p_send)
    landed(aout, a_send)
    landed(zout.at[:, pl.ds(0, groups - 1)], z_send)
    landed(qout, q_send)
    landed(fout, f_send)
    landed(yout, y_send)


def solution(mesh):
    groups, members = mesh.shape["grp"], mesh.shape["mem"]
    chips = members // 2
    pairs = chips // 2

    def body(volume, transfer_coef, group_order, member_order, active_mask):
        samples, image_rows, cols = volume.shape[2:]
        block_rows = image_rows // members
        stripes = block_rows // TILE_ROWS
        group_cols = cols // groups
        halves = min(HALVES, group_cols // LANES)
        part = group_cols // halves
        chunks = stripes * halves
        smem = pl.BlockSpec(memory_space=pltpu.SMEM)
        dma = pltpu.SemaphoreType.DMA

        def vmem(*shape):
            return pltpu.VMEM(shape, jnp.float32)

        tile = (TILE_ROWS, part * groups)
        piece = (TILE_ROWS, part)
        scratch = [
            vmem(stripes, samples, members, TILE_ROWS, cols),
            vmem(chunks, members, *tile),
            vmem(chunks, members, *tile),
            vmem(chunks, members, 3, *tile),
            vmem(chunks, chips, *tile),
            vmem(chunks, pairs - 1, *tile),
            vmem(chunks, 4 * chips + pairs, *tile),
            vmem(chunks, pairs, 3, *tile),
            vmem(chunks, pairs, 3, *tile),
            vmem(chunks, pairs, 3, *tile),
            vmem(chunks, *tile),
            vmem(chunks, pairs - 1, groups, *piece),
            vmem(chunks, groups, *piece),
            vmem(chunks, groups, pairs, *piece),
            vmem(chunks, groups, pairs, *piece),
            vmem(chunks, groups, 3 * pairs, *piece),
            vmem(chunks, (groups - 1) * 3 * (pairs - 1) + (pairs - 1) * groups, *piece),
            vmem(chunks, pairs - 1, 3, *piece),
            vmem(chunks, (groups - 1) * 3 + 3 * (pairs - 1), *piece),
            dma((stripes + members - 1,)),
            dma, dma((chunks,)),
            dma, dma, dma, dma((chunks,)),
            dma, dma((2,)),
            dma,
            dma, dma, dma((chunks,)),
            dma, dma((chunks,)),
        ]
        return pl.pallas_call(
            functools.partial(kernel, groups, members),
            out_shape=pltpu.VMEM((4, block_rows, group_cols), jnp.float32),
            in_specs=[smem, smem, smem, smem, pl.BlockSpec(memory_space=pl.ANY)],
            out_specs=pl.BlockSpec(memory_space=pltpu.VMEM),
            scratch_shapes=scratch,
            compiler_params=pltpu.CompilerParams(
                collective_id=0, has_side_effects=True, vmem_limit_bytes=60 * 1024 * 1024),
        )(transfer_coef, group_order, member_order, active_mask,
          volume.reshape(samples, members, block_rows, cols))

    in_specs = (P("grp", "mem", None, None, None), P(), P(), P(), P("grp", "mem"))
    out_specs = P(None, "mem", "grp")
    return jax.shard_map(body, mesh=mesh, in_specs=in_specs, out_specs=out_specs, check_vma=False)
```
